512 devices in a mesh: section: 4 (over y), band: 128 (over z, x, core).
Axes of the slice: x: 4, y: 4, z: 16, core: 2. Of those that a mesh axis runs over, the one named last changes fastest.
Arguments:
- control: bfloat16 [4, 512, 2, 128, 512], P('section', 'band'), may hold values from -6 to 6
- legendre: bfloat16 [512, 512, 512], P('band'), may hold values from -0.25 to 0.25
- spectral_sd: float32 [4, 512], P('section'), may hold values from 0.3 to 3
- vertical: bfloat16 [4, 128, 128], P('section'), may hold values from -0.5 to 0.5
- obs_lon: int32 [512, 1024], P('band'), may hold values from 0 to 1023
- obs_count: int32 [512], P('band'), may hold values from 1 to 1024, as said below
- kernels: bfloat16 [512, 1024, 128], P('band'), may hold values from 0 to 0.0039978027
- obs_value: float32 [512, 1024], P('band'), may hold values from -8 to 8
- obs_weight: float32 [512, 1024], P('band'), may hold values from 1 to 16
Outputs:
- gradient: bfloat16 [4, 512, 2, 128, 512], P('section', 'band')
- departures: float32 [512, 1024], P('band')
The draws below stay inside these ranges and needn't reach their ends.
Inputs may be any that keep to these rules, and one draw needn't show every extreme that they name: Slots 0 to obs_count - 1 of a latitude row hold its soundings, the others are empty; some row holds exactly 1024.
All inputs are finite; a program needn't handle non-finite values.
Results may differ from the reference program's by a relative error of at most 0.014.
Values may be sent and summed in bfloat16 or wider, within the bound.
No kernel may reach another device: no remote copies, remote signals or barrier semaphores. Data moves between devices by JAX's collectives and lax.ppermute only.
A program may use at most 64 MiB of HBM per device.

```python
import math
import jax
import jax.numpy as jnp
from jax import lax

M = 512
N = 512
NLAT = 512
NLON = 1024
LEV = 128
KROW = 1024
COMPONENTS = 4


def draw_obs_count(key, part):
    base_key = jax.random.fold_in(key, 7)
    first_key, second_key, row_key = jax.random.split(base_key, 3)
    first_draw = jax.random.randint(first_key, (NLAT,), 0, KROW)
    second_draw = jax.random.randint(second_key, (NLAT,), 0, KROW)
    counts = KROW - first_draw * second_draw // (4 * KROW)
    chosen = jax.random.randint(row_key, (), 0, NLAT)
    return jnp.where(jnp.arange(NLAT) == chosen, KROW, counts).astype(jnp.int32)


def set_ends(result, key, low, high):
    extent = result.shape
    spot = [jax.random.randint(jax.random.fold_in(key, axis), (), 0, extent[axis]) for axis in range(len(extent))]
    result = result.at[tuple(spot)].set(low)
    longest = extent.index(max(extent))
    spot[longest] = (spot[longest] + 1) % extent[longest]
    return result.at[tuple(spot)].set(high)


def levels(key, shape, shards, least, top_value):
    def one(axis_at, blocks):
        heights = jax.random.uniform(jax.random.fold_in(jax.random.fold_in(key, 6), axis_at), (blocks,), jnp.float32, least / len(shards), top_value / len(shards))
        return jnp.repeat(jnp.exp(heights), shape[axis_at] // blocks).reshape((-1,) + (1,) * (len(shape) - axis_at - 1))

    gain = one(*shards[0])
    for cut in shards[1:]:
        gain = gain * one(*cut)
    return gain


def bell_draw(rng, shape, scale, limit, cuts=(), held_as=jnp.bfloat16):
    factor_of = levels(rng, shape, cuts, -0.22, 0.18) if cuts else 1.0
    result = jax.random.normal(rng, shape, jnp.float32) * scale * factor_of
    return jnp.minimum(jnp.maximum(result, -limit), limit).astype(held_as)


def setup_inputs(seed: int = 0) -> dict:
    arg_keys = jax.random.split(jax.random.key(seed), 10)
    return {
        "control": bell_draw(arg_keys[0], (COMPONENTS, M, 2, LEV, N), 1.0, 6.0, ((0, 4), (1, 128))),
        "legendre": bell_draw(arg_keys[1], (M, N, NLAT), N ** -0.5, 0.25, ((0, 128),)),
        "spectral_sd": jnp.clip(jnp.exp(math.log(3.0) - 2.3025851 * jax.random.uniform(arg_keys[2], (COMPONENTS, N), jnp.float32) ** levels(arg_keys[2], (COMPONENTS, N), ((0, 4),), -0.2, 0.2)), 0.3, 3.0),
        "vertical": bell_draw(arg_keys[3], (COMPONENTS, LEV, LEV), LEV ** -0.5, 0.5, ((0, 4),)),
        "obs_lon": set_ends(jax.random.randint(arg_keys[4], (NLAT, KROW), 0, NLON), jax.random.fold_in(arg_keys[4], 1), 0, NLON - 1).astype(jnp.int32),
        "obs_count": draw_obs_count(jax.random.fold_in(arg_keys[9], 71), 0),
        "kernels": jnp.clip(0.0039978027 * jax.random.uniform(arg_keys[6], (NLAT, KROW, LEV), jnp.float32) ** levels(arg_keys[6], (NLAT, KROW, LEV), ((0, 128),), -0.2, 0.2), 0.0, 0.0039978027).astype(jnp.bfloat16),
        "obs_value": bell_draw(arg_keys[7], (NLAT, KROW), 2.0, 8.0, ((0, 128),), jnp.float32),
        "obs_weight": jnp.clip(jnp.exp(math.log(16.0) - 2.7725887 * jax.random.uniform(arg_keys[8], (NLAT, KROW), jnp.float32) ** levels(arg_keys[8], (NLAT, KROW), ((0, 128),), -0.2, 0.2)), 1.0, 16.0),
    }


def make_basis(longitude):
    wave_ids = jnp.arange(M, dtype=jnp.int32)
    phase_idx = (longitude[..., None] * wave_ids) % NLON
    angles = phase_idx.astype(jnp.float32) * (2.0 * math.pi / NLON)
    wave_weight = jnp.where(wave_ids == 0, 1.0, 2.0).astype(jnp.float32)
    fourier = jnp.stack([wave_weight * jnp.cos(angles), -wave_weight * jnp.sin(angles)], axis=-2)
    return fourier.astype(jnp.bfloat16)


def reference(control, legendre, spectral_sd, vertical, obs_lon, obs_count, kernels, obs_value, obs_weight):
    legendre_wide = legendre.astype(jnp.float32)

    def add_component(field_sum, inputs):
        coeffs, spread, mixing = inputs
        scaled = (coeffs.astype(jnp.float32) * spread).astype(jnp.bfloat16)
        spectral_rows = jnp.einsum('mnj,mrkn->mjrk', legendre_wide, scaled.astype(jnp.float32)).astype(jnp.bfloat16)
        fields = jnp.einsum('mjrk,lk->mjrl', spectral_rows.astype(jnp.float32), mixing.astype(jnp.float32)).astype(jnp.bfloat16)
        return field_sum + fields.astype(jnp.float32), None

    start_sum = jnp.zeros((M, NLAT, 2, LEV), jnp.float32)
    field_sum, _ = lax.scan(add_component, start_sum, (control, spectral_sd, vertical))
    row_fields = jnp.moveaxis(field_sum, 1, 0)

    def row_evolve(inputs):
        longitude, field_row, kern_row = inputs
        fourier = make_basis(longitude).astype(jnp.float32)
        columns = jnp.einsum('qrm,mrl->ql', fourier, field_row, precision=lax.Precision.HIGHEST)
        return jnp.sum(kern_row.astype(jnp.float32) * columns, axis=-1)

    evolved = lax.map(row_evolve, (obs_lon, row_fields, kernels))
    slot_ids = lax.broadcasted_iota(jnp.int32, (NLAT, KROW), 1)
    is_live = slot_ids < obs_count[:, None]
    departures = jnp.where(is_live, evolved - obs_value, jnp.float32(0.0))
    adjoint_columns = ((obs_weight * departures)[:, :, None] * kernels.astype(jnp.float32)).astype(jnp.bfloat16)

    def row_adjoint(inputs):
        longitude, adjoint_row = inputs
        fourier = make_basis(longitude).astype(jnp.float32)
        return jnp.einsum('qrm,ql->mrl', fourier, adjoint_row.astype(jnp.float32)).astype(jnp.bfloat16)

    adjoint_stack = lax.map(row_adjoint, (obs_lon, adjoint_columns))
    adjoint_fields = jnp.moveaxis(adjoint_stack, 0, 1).astype(jnp.float32)

    def component_gradient(inputs):
        coeffs, spread, mixing = inputs
        adjoint_rows = jnp.einsum('mjrl,lk->mjrk', adjoint_fields, mixing.astype(jnp.float32)).astype(jnp.bfloat16)
        back_terms = jnp.einsum('mjrk,mnj->mrkn', adjoint_rows.astype(jnp.float32), legendre_wide)
        return (coeffs.astype(jnp.float32) + spread * back_terms).astype(jnp.bfloat16)

    gradient = lax.map(component_gradient, (control, spectral_sd, vertical))
    return gradient, departures
```

```python
import math

import jax
import jax.numpy as jnp
from jax import lax
from jax.sharding import PartitionSpec as P

NLON = 1024
COARSE = 32


def turn(index):
    angle = (index & (NLON - 1)).astype(jnp.float32) * (2.0 * math.pi / NLON)
    return jnp.cos(angle), jnp.sin(angle)


def make_basis(longitude, waves):
    lon = longitude[None, :]
    fine = lax.broadcasted_iota(jnp.int32, (COARSE, 1), 0)
    coarse = lax.broadcasted_iota(jnp.int32, (waves // COARSE, 1), 0) * COARSE
    tables = turn(coarse * lon) + turn(fine * lon)
    cos_a, sin_a, cos_b, sin_b = lax.optimization_barrier(tables)
    cos_a, sin_a = 2.0 * cos_a[:, None, :], 2.0 * sin_a[:, None, :]
    cos_b, sin_b = cos_b[None], sin_b[None]
    wave_ids = lax.broadcasted_iota(jnp.int32, (waves // COARSE, COARSE, 1), 0) * COARSE
    wave_ids = wave_ids + lax.broadcasted_iota(jnp.int32, wave_ids.shape, 1)
    cos_m = jnp.where(wave_ids == 0, 1.0, cos_a * cos_b - sin_a * sin_b)
    sin_m = -(sin_a * cos_b + cos_a * sin_b)
    shape = (waves, longitude.shape[0])
    return cos_m.reshape(shape).astype(jnp.bfloat16), sin_m.reshape(shape).astype(jnp.bfloat16)


def make_local(sections, bands):
    def local(
        control, legendre, spectral_sd, vertical, obs_lon, obs_count, kernels, obs_value, obs_weight
    ):
        coeffs = control[0]
        spread = spectral_sd[0]
        mixing = vertical[0]
        waves_here, _, latitudes = legendre.shape
        levels = mixing.shape[0]
        waves = waves_here * bands
        here = lax.axis_index("section")
        longitude = lax.dynamic_index_in_dim(obs_lon, here, 0, keepdims=False)
        cos_m, sin_m = make_basis(longitude, waves)

        scaled = (coeffs.astype(jnp.float32) * spread).astype(jnp.bfloat16)
        spectral_rows = jnp.einsum(
            "mnj,mrkn->mjrk", legendre, scaled, preferred_element_type=jnp.float32
        ).astype(jnp.bfloat16)
        fields = jnp.einsum(
            "mjrk,lk->mjrl", spectral_rows, mixing, preferred_element_type=jnp.float32
        ).astype(jnp.bfloat16)
        fields = fields.reshape(waves_here, bands, sections, 2, levels).transpose(2, 1, 0, 3, 4)
        shares = lax.all_to_all(fields, "section", split_axis=0, concat_axis=0, tiled=True)
        field_sum = jnp.sum(shares.astype(jnp.float32), axis=0).astype(jnp.bfloat16)
        row_fields = lax.all_to_all(field_sum, "band", split_axis=0, concat_axis=0, tiled=True)
        row_fields = row_fields.reshape(waves, 2, levels)

        kern = lax.dynamic_index_in_dim(kernels, here, 0, keepdims=False)
        value = lax.dynamic_index_in_dim(obs_value, here, 0, keepdims=False)
        weight = lax.dynamic_index_in_dim(obs_weight, here, 0, keepdims=False)
        count = lax.dynamic_index_in_dim(obs_count, here, 0, keepdims=False)
        columns = jnp.einsum(
            "mq,ml->ql", cos_m, row_fields[:, 0], preferred_element_type=jnp.float32
        ) + jnp.einsum("mq,ml->ql", sin_m, row_fields[:, 1], preferred_element_type=jnp.float32)
        evolved = jnp.sum(kern.astype(jnp.float32) * columns, axis=-1)
        is_live = lax.broadcasted_iota(jnp.int32, evolved.shape, 0) < count
        departures = jnp.where(is_live, evolved - value, jnp.float32(0.0))
        adjoint_columns = ((weight * departures)[:, None] * kern.astype(jnp.float32)).astype(
            jnp.bfloat16
        )
        adjoint = [
            jnp.einsum("mq,ql->ml", basis, adjoint_columns, preferred_element_type=jnp.float32)
            for basis in (cos_m, sin_m)
        ]
        adjoint = jnp.stack(adjoint, axis=1).astype(jnp.bfloat16)
        adjoint = adjoint.reshape(bands, waves_here, 2, levels)
        back = lax.all_to_all(adjoint, "band", split_axis=0, concat_axis=0, tiled=True)
        piece1 = departures.astype(jnp.bfloat16)
        rest = departures - piece1.astype(jnp.float32)
        piece2 = rest.astype(jnp.bfloat16)
        piece3 = (rest - piece2.astype(jnp.float32)).astype(jnp.bfloat16)
        pieces = jnp.concatenate([piece1, piece2, piece3]).reshape(-1, levels)
        packet = jnp.concatenate([back.reshape(-1, levels), pieces], axis=0)
        packets = lax.all_to_all(
            jnp.broadcast_to(packet[None], (sections,) + packet.shape),
            "section", split_axis=0, concat_axis=0, tiled=True,
        )
        body = bands * waves_here * 2
        back_all = packets[:, :body].reshape(sections, bands, waves_here, 2, levels)
        parts = packets[:, body:].astype(jnp.float32).reshape(sections, 3, -1)
        all_departures = (parts[:, 2] + parts[:, 1]) + parts[:, 0]

        back_rows = jnp.einsum(
            "tbmrl,lk->tbmrk", back_all, mixing, preferred_element_type=jnp.float32
        ).astype(jnp.bfloat16)
        basis_rows = legendre.reshape(waves_here, -1, bands, sections)
        gradient_terms = jnp.einsum(
            "tbmrk,mnbt->mrkn", back_rows, basis_rows, preferred_element_type=jnp.float32
        )
        gradient = (coeffs.astype(jnp.float32) + spread * gradient_terms).astype(jnp.bfloat16)
        return (gradient[None], all_departures)

    return local


def solution(mesh):
    in_specs = (
        P("section", "band", None, None, None),
        P("band", None, None),
        P("section", None),
        P("section", None, None),
        P("band", None),
        P("band"),
        P("band", None, None),
        P("band", None),
        P("band", None),
    )
    out_specs = (P("section", "band", None, None, None), P("band", None))
    local = make_local(mesh.shape["section"], mesh.shape["band"])
    return jax.shard_map(local, mesh=mesh, in_specs=in_specs, out_specs=out_specs, check_vma=False)
```

```python
import functools
import math

import jax
import jax.numpy as jnp
from jax import lax
from jax.experimental import pallas as pl
from jax.experimental.pallas import tpu as pltpu
from jax.sharding import PartitionSpec as P

NLON = 1024
FINE = 64
F32 = jnp.float32
BF16 = jnp.bfloat16
MINOR_BOTH = (((1,), (1,)), ((), ()))


WHOLE = pl.BlockSpec(memory_space=pltpu.VMEM)
SCALAR = pl.BlockSpec(memory_space=pltpu.SMEM)
APART = pl.BlockSpec(memory_space=pl.ANY)


LIMIT = pltpu.CompilerParams(vmem_limit_bytes=16 << 20)


def made(shape, kind):
    return pltpu.VMEM(shape, kind)


def near(array):
    return pltpu.with_memory_space_constraint(array, pltpu.VMEM)


def view(ref, shape):
    return ref.reshape(shape)


def far(array):
    return pltpu.with_memory_space_constraint(array, pltpu.HBM)


def dot(a, b):
    return jnp.dot(a, b, preferred_element_type=F32)


def dot_minor(a, b):
    return lax.dot_general(a, b, MINOR_BOTH, preferred_element_type=F32)


def grouping(sections, bands):
    size = sections * bands
    shift = bands.bit_length() - 1
    place = lax.broadcasted_iota(jnp.int32, (size, size), 0)
    row = lax.broadcasted_iota(jnp.int32, (size, size), 1)
    home = sections * (place & (bands - 1)) + lax.shift_right_logical(place, shift)
    return jnp.where(home == row, 1.0, 0.0).astype(BF16)


def pull(pairs, sems):
    copies = [pltpu.make_async_copy(a, b, sems.at[i]) for i, (a, b) in enumerate(pairs)]
    for copy in copies:
        copy.start()
    return copies


def forward_body(
    sections, bands, control, legendre, spread, mixing, out,
    held, coeffs, basis, spreads, mixings, diagonal, sems,
):
    waves_here, pairs, _ = control.shape
    levels = mixing.shape[0]
    latitudes = legendre.shape[2]
    tile = 2 * waves_here
    order = [(spread, spreads), (mixing, mixings)]
    for m in range(waves_here):
        order += [(control.at[m], coeffs.at[m]), (legendre.at[m], basis.at[m])]
    copies = pull(order, sems)
    copies[0].wait()
    copies[1].wait()
    diagonal[...] = jnp.zeros_like(diagonal)
    for r in range(2):
        part = pl.ds(r * levels, levels)
        diagonal[part, part] = mixings[...]
    for m in range(waves_here):
        copies[2 + 2 * m].wait()
        copies[3 + 2 * m].wait()
        scaled = (coeffs[m].astype(F32) * spreads[...]).astype(BF16)
        rows = lax.dot_general(
            basis[m], scaled, (((0,), (1,)), ((), ())), preferred_element_type=F32
        ).astype(BF16)
        fields = dot_minor(rows, diagonal[...])
        for r in range(2):
            held[pl.ds(2 * m + r, latitudes, stride=tile), :] = fields[
                :, r * levels : (r + 1) * levels
            ]
    placed = view(held, (bands, sections, tile, levels))
    for t in range(sections):
        out[pl.ds(t * bands * tile, bands * tile), :] = (
            placed[:, t].reshape(bands * tile, levels).astype(BF16)
        )


def forward_fields(control, legendre, spread, mixing, sections, bands):
    waves_here, pairs, numbers = control.shape
    latitudes = legendre.shape[2]
    levels = mixing.shape[0]
    rows = latitudes * 2 * waves_here
    return pl.pallas_call(
        functools.partial(forward_body, sections, bands),
        in_specs=[APART] * 4,
        out_specs=WHOLE,
        out_shape=made((rows, levels), BF16),
        scratch_shapes=[
            pltpu.VMEM((rows, levels), F32),
            pltpu.VMEM(control.shape, BF16),
            pltpu.VMEM(legendre.shape, BF16),
            pltpu.VMEM(spread.shape, F32),
            pltpu.VMEM(mixing.shape, BF16),
            pltpu.VMEM((2 * levels, 2 * levels), BF16),
            pltpu.SemaphoreType.DMA((2 + 2 * waves_here,)),
        ],
        name="forward_fields",
        compiler_params=LIMIT,
    )(far(control), far(legendre), far(spread), far(mixing))


def turn(index):
    angle = (index & (NLON - 1)).astype(F32) * (2.0 * math.pi / NLON)
    return jnp.cos(angle), jnp.sin(angle)


def basis_body(here, obs_lon, by_wave):
    terms, _ = by_wave.shape
    lon = obs_lon[pl.ds(here[0], 1), :]
    fine = lax.broadcasted_iota(jnp.int32, (FINE, 1), 0)
    coarse = lax.broadcasted_iota(jnp.int32, (terms // FINE, 1), 0)
    fine_cos, fine_sin = turn(lax.shift_right_logical(fine, 1) * lon + (fine & 1) * (NLON // 4))
    coarse_cos, coarse_sin = turn(coarse * (FINE // 2) * lon)
    coarse_cos, coarse_sin = 2.0 * coarse_cos, 2.0 * coarse_sin
    for a in range(terms // FINE):
        block = coarse_cos[a : a + 1] * fine_cos - coarse_sin[a : a + 1] * fine_sin
        if a == 0:
            block = jnp.where(fine < 2, fine_cos, block)
        by_wave[pl.ds(a * FINE, FINE), :] = block.astype(BF16)


def make_basis(here, obs_lon, terms):
    return pl.pallas_call(
        basis_body,
        in_specs=[SCALAR, WHOLE],
        out_specs=WHOLE,
        out_shape=made((terms, obs_lon.shape[1]), BF16),
        name="make_basis",
        compiler_params=LIMIT,
    )(here, obs_lon)


def observe_body(
    here, count, by_wave, fields, kernels, value, weight, adjoint, pieces, kern, departures, sems
):
    copy = pull([(kernels.at[here[0]], kern)], sems)[0]
    columns = lax.dot_general(
        by_wave[...], fields[...], (((0,), (0,)), ((), ())), preferred_element_type=F32
    )
    slots, lanes = kern.shape
    half = lanes // 2
    line = pl.ds(here[0], 1)
    rows = [jnp.broadcast_to(part[line, :], (half, slots)) for part in (value, weight)]
    known = jnp.concatenate(rows, axis=0).T
    copy.wait()
    wide = kern[...].astype(F32)
    evolved = jnp.sum(wide * columns, axis=1, keepdims=True)
    slot = lax.broadcasted_iota(jnp.int32, evolved.shape, 0)
    departed = jnp.where(slot < count[here[0]], evolved - known[:, :1], 0.0)
    scaled = (known[:, half : half + 1] * departed * wide).astype(BF16)
    adjoint[...] = dot(by_wave[...], scaled).astype(BF16)
    diagonal = lax.broadcasted_iota(jnp.int32, (lanes, lanes), 0) == lax.broadcasted_iota(
        jnp.int32, (lanes, lanes), 1
    )
    for i in range(slots // lanes):
        spot = jnp.where(diagonal, departed[i * lanes : (i + 1) * lanes], 0.0)
        departures[pl.ds(i, 1), :] = jnp.sum(spot, axis=0, keepdims=True)
    rest = departures[...]
    size = rest.shape[0]
    for i in range(3):
        piece = rest.astype(BF16)
        pieces[pl.ds(i * size, size), :] = piece
        rest = rest - piece.astype(F32)


def observe(here, count, by_wave, fields, kernels, value, weight):
    _, slots, levels = kernels.shape
    return pl.pallas_call(
        observe_body,
        in_specs=[SCALAR, SCALAR, WHOLE, WHOLE, APART, WHOLE, WHOLE],
        out_specs=[WHOLE, WHOLE],
        out_shape=[made(fields.shape, BF16), made((3 * slots // levels, levels), BF16)],
        scratch_shapes=[
            pltpu.VMEM((slots, levels), BF16),
            pltpu.VMEM((slots // levels, levels), F32),
            pltpu.SemaphoreType.DMA((1,)),
        ],
        name="observe",
        compiler_params=LIMIT,
    )(here, count, near(by_wave), near(fields), far(kernels), near(value), near(weight))


def sum_body(parts, out):
    total = parts[0].astype(F32)
    for section in range(1, parts.shape[0]):
        total = total + parts[section].astype(F32)
    out[...] = total.astype(BF16)


def sum_sections(parts):
    return pl.pallas_call(
        sum_body,
        in_specs=[WHOLE],
        out_specs=WHOLE,
        out_shape=made(parts.shape[1:], BF16),
        name="sum_sections",
        compiler_params=LIMIT,
    )(near(parts))


def regroup_body(sections, bands, legendre, out):
    group = grouping(sections, bands)
    for m in range(legendre.shape[0]):
        out[m] = dot_minor(legendre[m], group).astype(BF16)


def regroup(legendre, sections, bands):
    return pl.pallas_call(
        functools.partial(regroup_body, sections, bands),
        in_specs=[WHOLE],
        out_specs=WHOLE,
        out_shape=jax.ShapeDtypeStruct(legendre.shape, BF16),
        name="regroup",
        compiler_params=LIMIT,
    )(legendre)


def pack_body(body, pieces, out):
    rows = body.shape[0]
    for section in range(out.shape[0]):
        out[section, pl.ds(0, rows), :] = body[...]
        out[section, pl.ds(rows, pieces.shape[0]), :] = pieces[...]


def pack(body, pieces, sections):
    rows = body.shape[0] + pieces.shape[0]
    return pl.pallas_call(
        pack_body,
        in_specs=[WHOLE, WHOLE],
        out_specs=WHOLE,
        out_shape=made((sections, rows, body.shape[1]), BF16),
        name="pack",
        compiler_params=LIMIT,
    )(near(body), near(pieces))


def backward_body(packets, grouped, control, spread, mixing, out, departures, held, ready, sems):
    sections, _, levels = packets.shape
    waves_here = grouped.shape[0]
    latitudes = grouped.shape[2]
    tile = 2 * waves_here
    size = latitudes // sections * tile
    mixing_t = mixing[...].astype(F32).T.astype(BF16)
    lines = departures.shape[1] // levels
    for t in range(sections):
        held[pl.ds(t * size, size), :] = packets[t, pl.ds(0, size), :].astype(F32)
        parts = [packets[t, pl.ds(size + i * lines, lines), :].astype(F32) for i in range(3)]
        whole = (parts[2] + parts[1]) + parts[0]
        for i in range(lines):
            departures[pl.ds(t, 1), pl.ds(i * levels, levels)] = whole[i : i + 1]
    leaving = []
    for m in range(waves_here):
        rows = [held[pl.ds(2 * m + r, latitudes, stride=tile), :].astype(BF16) for r in range(2)]
        terms = dot(grouped[m], jnp.concatenate(rows, axis=1)).astype(BF16)
        for r in range(2):
            part = pl.ds(r * levels, levels)
            total = dot_minor(mixing_t, terms[:, r * levels : (r + 1) * levels])
            ready[m, part, :] = (control[m, part, :].astype(F32) + spread[...] * total).astype(BF16)
        copy = pltpu.make_async_copy(ready.at[m], out.at[m], sems.at[m])
        copy.start()
        leaving.append(copy)
    for copy in leaving:
        copy.wait()


def backward_gradient(packets, grouped, control, spread, mixing, slots):
    sections, _, levels = packets.shape
    waves_here, _, latitudes = grouped.shape
    return pl.pallas_call(
        backward_body,
        in_specs=[WHOLE] * 5,
        out_specs=[APART, WHOLE],
        out_shape=[
            jax.ShapeDtypeStruct(control.shape, BF16),
            jax.ShapeDtypeStruct((sections, slots), F32),
        ],
        scratch_shapes=[
            pltpu.VMEM((latitudes * 2 * waves_here, levels), F32),
            pltpu.VMEM(control.shape, BF16),
            pltpu.SemaphoreType.DMA((waves_here,)),
        ],
        name="backward_gradient",
        compiler_params=LIMIT,
    )(near(packets), near(grouped), near(control), near(spread), near(mixing))


def make_local(sections, bands):
    def local(
        control, legendre, spectral_sd, vertical, obs_lon, obs_count, kernels, obs_value, obs_weight
    ):
        mixing = vertical[0]
        waves_here, numbers, latitudes = legendre.shape
        levels = mixing.shape[0]
        tile = 2 * waves_here
        terms = tile * bands
        slots = obs_lon.shape[1]
        here = lax.axis_index("section").astype(jnp.int32)
        coeffs = control.reshape(waves_here, 2 * levels, numbers)

        fields = forward_fields(coeffs, legendre, spectral_sd, mixing, sections, bands)
        shares = lax.all_to_all(
            fields.reshape(sections, bands, tile, levels),
            "section", split_axis=0, concat_axis=0, tiled=True,
        )
        field_sum = sum_sections(shares.reshape(sections, terms, levels))
        row_fields = lax.all_to_all(
            field_sum.reshape(bands, tile, levels), "band", split_axis=0, concat_axis=0, tiled=True
        )

        by_wave = make_basis(here[None], obs_lon, terms)
        grouped = regroup(legendre, sections, bands)
        row_fields, by_wave, grouped = lax.optimization_barrier((row_fields, by_wave, grouped))
        adjoint, pieces = observe(
            here[None], obs_count, by_wave, row_fields.reshape(terms, levels),
            kernels, obs_value, obs_weight,
        )
        back = lax.all_to_all(
            adjoint.reshape(bands, tile, levels), "band", split_axis=0, concat_axis=0, tiled=True
        )
        packets = lax.all_to_all(
            pack(back.reshape(terms, levels), pieces, sections),
            "section", split_axis=0, concat_axis=0, tiled=True,
        )
        gradient, all_departures = backward_gradient(
            packets, grouped, coeffs, spectral_sd, mixing, slots
        )
        return (gradient.reshape(control.shape), all_departures)

    return local


def solution(mesh):
    in_specs = (
        P("section", "band", None, None, None),
        P("band", None, None),
        P("section", None),
        P("section", None, None),
        P("band", None),
        P("band"),
        P("band", None, None),
        P("band", None),
        P("band", None),
    )
    out_specs = (P("section", "band", None, None, None), P("band", None))
    local = make_local(mesh.shape["section"], mesh.shape["band"])
    return jax.shard_map(local, mesh=mesh, in_specs=in_specs, out_specs=out_specs, check_vma=False)
```

```python
import functools
import math

import jax
import jax.numpy as jnp
from jax import lax
from jax.experimental import pallas as pl
from jax.experimental.pallas import tpu as pltpu
from jax.sharding import PartitionSpec as P

NLON = 1024
FINE = 64
F32 = jnp.float32
BF16 = jnp.bfloat16
MINOR_BOTH = (((1,), (1,)), ((), ()))


WHOLE = pl.BlockSpec(memory_space=pltpu.VMEM)
SCALAR = pl.BlockSpec(memory_space=pltpu.SMEM)
APART = pl.BlockSpec(memory_space=pl.ANY)


LIMIT = pltpu.CompilerParams(vmem_limit_bytes=16 << 20)


def made(shape, kind):
    return pltpu.VMEM(shape, kind)


def near(array):
    return pltpu.with_memory_space_constraint(array, pltpu.VMEM)


def view(ref, shape):
    return ref.reshape(shape)


def far(array):
    return pltpu.with_memory_space_constraint(array, pltpu.HBM)


def dot(a, b):
    return jnp.dot(a, b, preferred_element_type=F32)


def dot_minor(a, b):
    return lax.dot_general(a, b, MINOR_BOTH, preferred_element_type=F32)


def grouping(sections, bands):
    size = sections * bands
    shift = bands.bit_length() - 1
    place = lax.broadcasted_iota(jnp.int32, (size, size), 0)
    row = lax.broadcasted_iota(jnp.int32, (size, size), 1)
    home = sections * (place & (bands - 1)) + lax.shift_right_logical(place, shift)
    return jnp.where(home == row, 1.0, 0.0).astype(BF16)


def pull(pairs, sems):
    copies = [pltpu.make_async_copy(a, b, sems.at[i]) for i, (a, b) in enumerate(pairs)]
    for copy in copies:
        copy.start()
    return copies


def forward_body(
    sections, bands, control, legendre, spread, mixing, out,
    held, coeffs, basis, spreads, mixings, diagonal, sems,
):
    waves_here, pairs, _ = control.shape
    levels = mixing.shape[0]
    latitudes = legendre.shape[2]
    tile = 2 * waves_here
    order = [(spread, spreads), (mixing, mixings)]
    for m in range(waves_here):
        order += [(control.at[m], coeffs.at[m]), (legendre.at[m], basis.at[m])]
    copies = [pltpu.make_async_copy(a, b, sems.at[i]) for i, (a, b) in enumerate(order)]
    for copy in copies[:6]:
        copy.start()
    copies[0].wait()
    copies[1].wait()
    diagonal[...] = jnp.zeros_like(diagonal)
    for r in range(2):
        part = pl.ds(r * levels, levels)
        diagonal[part, part] = mixings[...]
    for m in range(waves_here):
        copies[2 + 2 * m].wait()
        copies[3 + 2 * m].wait()
        for copy in copies[6 + 2 * m : 8 + 2 * m]:
            copy.start()
        scaled = (coeffs[m].astype(F32) * spreads[...]).astype(BF16)
        rows = lax.dot_general(
            basis[m], scaled, (((0,), (1,)), ((), ())), preferred_element_type=F32
        ).astype(BF16)
        fields = dot_minor(rows, diagonal[...])
        for r in range(2):
            held[pl.ds(2 * m + r, latitudes, stride=tile), :] = fields[
                :, r * levels : (r + 1) * levels
            ]
    placed = view(held, (bands, sections, tile, levels))
    for t in range(sections):
        out[pl.ds(t * bands * tile, bands * tile), :] = (
            placed[:, t].reshape(bands * tile, levels).astype(BF16)
        )


def forward_fields(control, legendre, spread, mixing, sections, bands):
    waves_here, pairs, numbers = control.shape
    latitudes = legendre.shape[2]
    levels = mixing.shape[0]
    rows = latitudes * 2 * waves_here
    return pl.pallas_call(
        functools.partial(forward_body, sections, bands),
        in_specs=[APART] * 4,
        out_specs=WHOLE,
        out_shape=made((rows, levels), BF16),
        scratch_shapes=[
            pltpu.VMEM((rows, levels), F32),
            pltpu.VMEM(control.shape, BF16),
            pltpu.VMEM(legendre.shape, BF16),
            pltpu.VMEM(spread.shape, F32),
            pltpu.VMEM(mixing.shape, BF16),
            pltpu.VMEM((2 * levels, 2 * levels), BF16),
            pltpu.SemaphoreType.DMA((2 + 2 * waves_here,)),
        ],
        name="forward_fields",
        compiler_params=LIMIT,
    )(far(control), far(legendre), far(spread), far(mixing))


def turn(index):
    angle = (index & (NLON - 1)).astype(F32) * (2.0 * math.pi / NLON)
    return jnp.cos(angle), jnp.sin(angle)


def basis_body(here, count, obs_lon, value, weight, kernels, by_wave, turned, lines, kern, sems):
    copy = pull([(kernels.at[here[0]], kern)], sems)[0]
    terms, slots = by_wave.shape
    line = pl.ds(here[0], 1)
    lon = obs_lon[line, :]
    fine = lax.broadcasted_iota(jnp.int32, (FINE, 1), 0)
    coarse = lax.broadcasted_iota(jnp.int32, (terms // FINE, 1), 0)
    fine_cos, fine_sin = turn(lax.shift_right_logical(fine, 1) * lon + (fine & 1) * (NLON // 4))
    coarse_cos, coarse_sin = turn(coarse * (FINE // 2) * lon)
    coarse_cos, coarse_sin = 2.0 * coarse_cos, 2.0 * coarse_sin
    for a in range(terms // FINE):
        block = coarse_cos[a : a + 1] * fine_cos - coarse_sin[a : a + 1] * fine_sin
        if a == 0:
            block = jnp.where(fine < 2, fine_cos, block)
        by_wave[pl.ds(a * FINE, FINE), :] = block.astype(BF16)
    slot = lax.broadcasted_iota(jnp.int32, (1, slots), 1)
    lines[pl.ds(0, 1), :] = value[line, :]
    lines[pl.ds(1, 1), :] = weight[line, :]
    lines[pl.ds(2, 1), :] = jnp.where(slot < count[here[0]], 1.0, 0.0)
    levels = kern.shape[1]
    eye = lax.broadcasted_iota(jnp.int32, (levels, levels), 0) == lax.broadcasted_iota(
        jnp.int32, (levels, levels), 1
    )
    copy.wait()
    turned[...] = dot_minor(jnp.where(eye, 1.0, 0.0).astype(BF16), kern[...]).astype(BF16)


def make_basis(here, count, obs_lon, value, weight, kernels, terms):
    _, slots, levels = kernels.shape
    return pl.pallas_call(
        basis_body,
        in_specs=[SCALAR, SCALAR, WHOLE, WHOLE, WHOLE, APART],
        out_specs=[WHOLE] * 3,
        out_shape=[
            made((terms, slots), BF16),
            made((levels, slots), BF16),
            made((8, slots), F32),
        ],
        scratch_shapes=[pltpu.VMEM((slots, levels), BF16), pltpu.SemaphoreType.DMA((1,))],
        name="make_basis",
        compiler_params=LIMIT,
    )(here, count, obs_lon, value, weight, far(kernels))


def observe_body(by_wave, fields, kern, lines, adjoint, pieces, departures):
    columns = dot(fields[...].T, by_wave[...])
    wide = kern[...].astype(F32)
    evolved = jnp.sum(wide * columns, axis=0, keepdims=True)
    departed = jnp.where(lines[pl.ds(2, 1), :] > 0.5, evolved - lines[pl.ds(0, 1), :], 0.0)
    scaled = (lines[pl.ds(1, 1), :] * departed * wide).astype(BF16)
    adjoint[...] = dot_minor(scaled, by_wave[...]).T.astype(BF16)
    size, lanes = departures.shape
    for i in range(size):
        departures[pl.ds(i, 1), :] = departed[:, i * lanes : (i + 1) * lanes]
    rest = departures[...]
    for i in range(3):
        piece = rest.astype(BF16)
        pieces[pl.ds(i * size, size), :] = piece
        rest = rest - piece.astype(F32)


def observe(by_wave, fields, kern, lines):
    levels, slots = kern.shape
    return pl.pallas_call(
        observe_body,
        in_specs=[WHOLE] * 4,
        out_specs=[WHOLE, WHOLE],
        out_shape=[made(fields.shape, BF16), made((3 * slots // levels, levels), BF16)],
        scratch_shapes=[pltpu.VMEM((slots // levels, levels), F32)],
        name="observe",
        compiler_params=LIMIT,
    )(near(by_wave), near(fields), near(kern), near(lines))


def sum_body(parts, out):
    total = parts[0].astype(F32)
    for section in range(1, parts.shape[0]):
        total = total + parts[section].astype(F32)
    out[...] = total.astype(BF16)


def sum_sections(parts):
    return pl.pallas_call(
        sum_body,
        in_specs=[WHOLE],
        out_specs=WHOLE,
        out_shape=made(parts.shape[1:], BF16),
        name="sum_sections",
        compiler_params=LIMIT,
    )(near(parts))


def regroup_body(sections, bands, legendre, out):
    group = grouping(sections, bands)
    for m in range(legendre.shape[0]):
        out[m] = dot_minor(legendre[m], group).astype(BF16)


def regroup(legendre, sections, bands):
    return pl.pallas_call(
        functools.partial(regroup_body, sections, bands),
        in_specs=[WHOLE],
        out_specs=WHOLE,
        out_shape=jax.ShapeDtypeStruct(legendre.shape, BF16),
        name="regroup",
        compiler_params=LIMIT,
    )(legendre)


def pack_body(tile, body, pieces, out, held):
    held[...] = body[...].astype(F32)
    rows = body.shape[0]
    run = rows // tile
    for i in range(tile):
        block = held[pl.ds(i, run, stride=tile), :].astype(BF16)
        for section in range(out.shape[0]):
            out[section, pl.ds(i * run, run), :] = block
    for section in range(out.shape[0]):
        out[section, pl.ds(rows, pieces.shape[0]), :] = pieces[...]


def pack(body, pieces, sections, tile):
    rows = body.shape[0] + pieces.shape[0]
    return pl.pallas_call(
        functools.partial(pack_body, tile),
        in_specs=[WHOLE, WHOLE],
        out_specs=WHOLE,
        out_shape=made((sections, rows, body.shape[1]), BF16),
        scratch_shapes=[pltpu.VMEM(body.shape, F32)],
        name="pack",
        compiler_params=LIMIT,
    )(near(body), near(pieces))


def backward_body(
    packets, grouped, control, spread, mixing, out, all_departures, ready, departures, sems
):
    sections, _, levels = packets.shape
    waves_here = grouped.shape[0]
    run = grouped.shape[2] // sections
    size = run * 2 * waves_here
    mixing_t = mixing[...].astype(F32).T.astype(BF16)
    lines = departures.shape[1] // levels
    for t in range(sections):
        parts = [packets[t, pl.ds(size + i * lines, lines), :].astype(F32) for i in range(3)]
        whole = (parts[2] + parts[1]) + parts[0]
        for i in range(lines):
            departures[pl.ds(t, 1), pl.ds(i * levels, levels)] = whole[i : i + 1]
    leaving = pull([(departures, all_departures)], sems)
    for m in range(waves_here):
        rows = [
            jnp.concatenate([packets[t, pl.ds((2 * m + r) * run, run), :] for t in range(sections)])
            for r in range(2)
        ]
        terms = dot(grouped[m], jnp.concatenate(rows, axis=1)).astype(BF16)
        for r in range(2):
            part = pl.ds(r * levels, levels)
            total = dot_minor(mixing_t, terms[:, r * levels : (r + 1) * levels])
            ready[m, part, :] = (control[m, part, :].astype(F32) + spread[...] * total).astype(BF16)
        copy = pltpu.make_async_copy(ready.at[m], out.at[m], sems.at[m + 1])
        copy.start()
        leaving.append(copy)
    for copy in leaving:
        copy.wait()


def backward_gradient(packets, grouped, control, spread, mixing, slots):
    sections = packets.shape[0]
    waves_here = grouped.shape[0]
    return pl.pallas_call(
        backward_body,
        in_specs=[WHOLE] * 5,
        out_specs=[APART, APART],
        out_shape=[
            jax.ShapeDtypeStruct(control.shape, BF16),
            jax.ShapeDtypeStruct((sections, slots), F32),
        ],
        scratch_shapes=[
            pltpu.VMEM(control.shape, BF16),
            pltpu.VMEM((sections, slots), F32),
            pltpu.SemaphoreType.DMA((1 + waves_here,)),
        ],
        name="backward_gradient",
        compiler_params=LIMIT,
    )(near(packets), near(grouped), near(control), near(spread), near(mixing))


def make_local(sections, bands):
    def local(
        control, legendre, spectral_sd, vertical, obs_lon, obs_count, kernels, obs_value, obs_weight
    ):
        mixing = vertical[0]
        waves_here, numbers, latitudes = legendre.shape
        levels = mixing.shape[0]
        tile = 2 * waves_here
        terms = tile * bands
        slots = obs_lon.shape[1]
        here = lax.axis_index("section").astype(jnp.int32)
        coeffs = control.reshape(waves_here, 2 * levels, numbers)

        fields = forward_fields(coeffs, legendre, spectral_sd, mixing, sections, bands)
        shares = lax.all_to_all(
            fields.reshape(sections, bands, tile, levels),
            "section", split_axis=0, concat_axis=0, tiled=True,
        )
        field_sum = sum_sections(shares.reshape(sections, terms, levels))
        row_fields = lax.all_to_all(
            field_sum.reshape(bands, tile, levels), "band", split_axis=0, concat_axis=0, tiled=True
        )

        tables = make_basis(
            here[None], obs_count, obs_lon, obs_value, obs_weight, kernels, terms
        )
        grouped = regroup(legendre, sections, bands)
        row_fields, tables, grouped = lax.optimization_barrier((row_fields, tables, grouped))
        by_wave, kern, lines = tables
        adjoint, pieces = observe(by_wave, row_fields.reshape(terms, levels), kern, lines)
        back = lax.all_to_all(
            adjoint.reshape(bands, tile, levels), "band", split_axis=0, concat_axis=0, tiled=True
        )
        packets = lax.all_to_all(
            pack(back.reshape(terms, levels), pieces, sections, tile),
            "section", split_axis=0, concat_axis=0, tiled=True,
        )
        gradient, all_departures = backward_gradient(
            packets, grouped, coeffs, spectral_sd, mixing, slots
        )
        return (gradient.reshape(control.shape), all_departures)

    return local


def solution(mesh):
    in_specs = (
        P("section", "band", None, None, None),
        P("band", None, None),
        P("section", None),
        P("section", None, None),
        P("band", None),
        P("band"),
        P("band", None, None),
        P("band", None),
        P("band", None),
    )
    out_specs = (P("section", "band", None, None, None), P("band", None))
    local = make_local(mesh.shape["section"], mesh.shape["band"])
    return jax.shard_map(local, mesh=mesh, in_specs=in_specs, out_specs=out_specs, check_vma=False)
```

```python
import functools
import math

import jax
import jax.numpy as jnp
from jax import lax
from jax.experimental import pallas as pl
from jax.experimental.pallas import tpu as pltpu
from jax.sharding import PartitionSpec as P

NLON = 1024
FINE = 64
F32 = jnp.float32
BF16 = jnp.bfloat16
MINOR_BOTH = (((1,), (1,)), ((), ()))


WHOLE = pl.BlockSpec(memory_space=pltpu.VMEM)
SCALAR = pl.BlockSpec(memory_space=pltpu.SMEM)
APART = pl.BlockSpec(memory_space=pl.ANY)


LIMIT = pltpu.CompilerParams(vmem_limit_bytes=16 << 20)


def made(shape, kind):
    return pltpu.VMEM(shape, kind)


def near(array):
    return pltpu.with_memory_space_constraint(array, pltpu.VMEM)


def view(ref, shape):
    return ref.reshape(shape)


def far(array):
    return pltpu.with_memory_space_constraint(array, pltpu.HBM)


def dot(a, b):
    return jnp.dot(a, b, preferred_element_type=F32)


def dot_minor(a, b):
    return lax.dot_general(a, b, MINOR_BOTH, preferred_element_type=F32)


def grouping(sections, bands):
    size = sections * bands
    shift = bands.bit_length() - 1
    place = lax.broadcasted_iota(jnp.int32, (size, size), 0)
    row = lax.broadcasted_iota(jnp.int32, (size, size), 1)
    home = sections * (place & (bands - 1)) + lax.shift_right_logical(place, shift)
    return jnp.where(home == row, 1.0, 0.0).astype(BF16)


def pull(pairs, sems):
    copies = [pltpu.make_async_copy(a, b, sems.at[i]) for i, (a, b) in enumerate(pairs)]
    for copy in copies:
        copy.start()
    return copies


def forward_body(
    sections, bands, control, legendre, spread, mixing, out,
    held, coeffs, basis, spreads, mixings, diagonal, sems,
):
    waves_here, pairs, _ = control.shape
    levels = mixing.shape[0]
    latitudes = legendre.shape[2]
    tile = 2 * waves_here
    order = [(spread, spreads), (mixing, mixings)]
    for m in range(waves_here):
        order += [(control.at[m], coeffs.at[m]), (legendre.at[m], basis.at[m])]
    copies = [pltpu.make_async_copy(a, b, sems.at[i]) for i, (a, b) in enumerate(order)]
    for copy in copies[:6]:
        copy.start()
    copies[0].wait()
    copies[1].wait()
    diagonal[...] = jnp.zeros_like(diagonal)
    for r in range(2):
        part = pl.ds(r * levels, levels)
        diagonal[part, part] = mixings[...]
    for m in range(waves_here):
        copies[2 + 2 * m].wait()
        copies[3 + 2 * m].wait()
        for copy in copies[6 + 2 * m : 8 + 2 * m]:
            copy.start()
        scaled = (coeffs[m].astype(F32) * spreads[...]).astype(BF16)
        rows = lax.dot_general(
            basis[m], scaled, (((0,), (1,)), ((), ())), preferred_element_type=F32
        ).astype(BF16)
        fields = dot_minor(rows, diagonal[...])
        for r in range(2):
            held[pl.ds(2 * m + r, latitudes, stride=tile), :] = fields[
                :, r * levels : (r + 1) * levels
            ]
    placed = view(held, (bands, sections, tile, levels))
    for t in range(sections):
        out[pl.ds(t * bands * tile, bands * tile), :] = (
            placed[:, t].reshape(bands * tile, levels).astype(BF16)
        )


def forward_fields(control, legendre, spread, mixing, sections, bands):
    waves_here, pairs, numbers = control.shape
    latitudes = legendre.shape[2]
    levels = mixing.shape[0]
    rows = latitudes * 2 * waves_here
    return pl.pallas_call(
        functools.partial(forward_body, sections, bands),
        in_specs=[APART] * 4,
        out_specs=WHOLE,
        out_shape=made((rows, levels), BF16),
        scratch_shapes=[
            pltpu.VMEM((rows, levels), F32),
            pltpu.VMEM(control.shape, BF16),
            pltpu.VMEM(legendre.shape, BF16),
            pltpu.VMEM(spread.shape, F32),
            pltpu.VMEM(mixing.shape, BF16),
            pltpu.VMEM((2 * levels, 2 * levels), BF16),
            pltpu.SemaphoreType.DMA((2 + 2 * waves_here,)),
        ],
        name="forward_fields",
        compiler_params=LIMIT,
    )(far(control), far(legendre), far(spread), far(mixing))


def turn(index):
    angle = (index & (NLON - 1)).astype(F32) * (2.0 * math.pi / NLON)
    return jnp.cos(angle), jnp.sin(angle)


def basis_body(here, count, obs_lon, value, weight, kernels, by_wave, turned, lines, kern, sems):
    copy = pull([(kernels.at[here[0]], kern)], sems)[0]
    terms, slots = by_wave.shape
    line = pl.ds(here[0], 1)
    lon = obs_lon[line, :]
    fine = lax.broadcasted_iota(jnp.int32, (FINE, 1), 0)
    coarse = lax.broadcasted_iota(jnp.int32, (terms // FINE, 1), 0)
    fine_cos, fine_sin = turn(lax.shift_right_logical(fine, 1) * lon + (fine & 1) * (NLON // 4))
    coarse_cos, coarse_sin = turn(coarse * (FINE // 2) * lon)
    coarse_cos, coarse_sin = 2.0 * coarse_cos, 2.0 * coarse_sin
    for a in range(terms // FINE):
        block = coarse_cos[a : a + 1] * fine_cos - coarse_sin[a : a + 1] * fine_sin
        if a == 0:
            block = jnp.where(fine < 2, fine_cos, block)
        by_wave[pl.ds(a * FINE, FINE), :] = block.astype(BF16)
    slot = lax.broadcasted_iota(jnp.int32, (1, slots), 1)
    lines[pl.ds(0, 1), :] = value[line, :]
    lines[pl.ds(1, 1), :] = weight[line, :]
    lines[pl.ds(2, 1), :] = jnp.where(slot < count[here[0]], 1.0, 0.0)
    levels = kern.shape[1]
    eye = lax.broadcasted_iota(jnp.int32, (levels, levels), 0) == lax.broadcasted_iota(
        jnp.int32, (levels, levels), 1
    )
    copy.wait()
    turned[...] = dot_minor(jnp.where(eye, 1.0, 0.0).astype(BF16), kern[...]).astype(BF16)


def make_basis(here, count, obs_lon, value, weight, kernels, terms):
    _, slots, levels = kernels.shape
    return pl.pallas_call(
        basis_body,
        in_specs=[SCALAR, SCALAR, WHOLE, WHOLE, WHOLE, APART],
        out_specs=[WHOLE] * 3,
        out_shape=[
            made((terms, slots), BF16),
            made((levels, slots), BF16),
            made((8, slots), F32),
        ],
        scratch_shapes=[pltpu.VMEM((slots, levels), BF16), pltpu.SemaphoreType.DMA((1,))],
        name="make_basis",
        compiler_params=LIMIT,
    )(here, count, obs_lon, value, weight, far(kernels))


def observe_body(by_wave, fields, kern, lines, adjoint, pieces, departures):
    columns = dot(fields[...].T, by_wave[...])
    wide = kern[...].astype(F32)
    evolved = jnp.sum(wide * columns, axis=0, keepdims=True)
    departed = jnp.where(lines[pl.ds(2, 1), :] > 0.5, evolved - lines[pl.ds(0, 1), :], 0.0)
    scaled = (lines[pl.ds(1, 1), :] * departed * wide).astype(BF16)
    adjoint[...] = dot_minor(scaled, by_wave[...]).T.astype(BF16)
    size, lanes = departures.shape
    for i in range(size):
        departures[pl.ds(i, 1), :] = departed[:, i * lanes : (i + 1) * lanes]
    rest = departures[...]
    for i in range(3):
        piece = rest.astype(BF16)
        pieces[pl.ds(i * size, size), :] = piece
        rest = rest - piece.astype(F32)


def observe(by_wave, fields, kern, lines, lanes):
    _, slots = kern.shape
    return pl.pallas_call(
        observe_body,
        in_specs=[WHOLE] * 4,
        out_specs=[WHOLE, WHOLE],
        out_shape=[made(fields.shape, BF16), made((3 * slots // lanes, lanes), BF16)],
        scratch_shapes=[pltpu.VMEM((slots // lanes, lanes), F32)],
        name="observe",
        compiler_params=LIMIT,
    )(near(by_wave), near(fields), near(kern), near(lines))


def sum_body(parts, out):
    total = parts[0].astype(F32)
    for section in range(1, parts.shape[0]):
        total = total + parts[section].astype(F32)
    out[...] = total.astype(BF16)


def sum_sections(parts):
    return pl.pallas_call(
        sum_body,
        in_specs=[WHOLE],
        out_specs=WHOLE,
        out_shape=made(parts.shape[1:], BF16),
        name="sum_sections",
        compiler_params=LIMIT,
    )(near(parts))


def regroup_body(sections, bands, legendre, out):
    group = grouping(sections, bands)
    for m in range(legendre.shape[0]):
        out[m] = dot_minor(group, legendre[m]).astype(BF16)


def regroup(legendre, sections, bands):
    waves_here, numbers, latitudes = legendre.shape
    return pl.pallas_call(
        functools.partial(regroup_body, sections, bands),
        in_specs=[WHOLE],
        out_specs=WHOLE,
        out_shape=jax.ShapeDtypeStruct((waves_here, latitudes, numbers), BF16),
        name="regroup",
        compiler_params=LIMIT,
    )(legendre)


def pack_body(tile, body, pieces, out, held):
    held[...] = body[...].astype(F32)
    rows, levels = body.shape
    run = rows // tile
    size = tile * levels
    for i in range(tile):
        block = held[pl.ds(i, run, stride=tile), :].T.astype(BF16)
        for section in range(out.shape[0]):
            out[section, pl.ds(i * levels, levels), :] = block
    for section in range(out.shape[0]):
        out[section, pl.ds(size, pieces.shape[0]), :] = pieces[...]


def pack(body, pieces, sections, tile):
    levels = body.shape[1]
    rows = tile * levels + pieces.shape[0]
    return pl.pallas_call(
        functools.partial(pack_body, tile),
        in_specs=[WHOLE, WHOLE],
        out_specs=WHOLE,
        out_shape=made((sections, rows, body.shape[0] // tile), BF16),
        scratch_shapes=[pltpu.VMEM(body.shape, F32)],
        name="pack",
        compiler_params=LIMIT,
    )(near(body), near(pieces))


def backward_body(
    packets, grouped, control, spread, mixing, out, all_departures,
    ready, departures, diagonal, sems,
):
    sections, _, lanes = packets.shape
    waves_here = grouped.shape[0]
    levels = mixing.shape[0]
    size = levels * 2 * waves_here
    lines = departures.shape[1] // lanes
    for t in range(sections):
        parts = [packets[t, pl.ds(size + i * lines, lines), :].astype(F32) for i in range(3)]
        whole = (parts[2] + parts[1]) + parts[0]
        for i in range(lines):
            departures[pl.ds(t, 1), pl.ds(i * lanes, lanes)] = whole[i : i + 1]
    leaving = pull([(departures, all_departures)], sems)
    mixing_t = mixing[...].astype(F32).T.astype(BF16)
    diagonal[...] = jnp.zeros_like(diagonal)
    for r in range(2):
        part = pl.ds(r * levels, levels)
        diagonal[part, part] = mixing_t
    for m in range(waves_here):
        part = pl.ds(2 * m * levels, 2 * levels)
        turned = jnp.concatenate([packets[t, part, :] for t in range(sections)], axis=1)
        terms = dot(turned, grouped[m]).astype(BF16)
        total = dot(diagonal[...], terms)
        ready[m] = (control[m].astype(F32) + spread[...] * total).astype(BF16)
        copy = pltpu.make_async_copy(ready.at[m], out.at[m], sems.at[m + 1])
        copy.start()
        leaving.append(copy)
    for copy in leaving:
        copy.wait()


def backward_gradient(packets, grouped, control, spread, mixing, slots):
    sections = packets.shape[0]
    waves_here = grouped.shape[0]
    return pl.pallas_call(
        backward_body,
        in_specs=[WHOLE] * 5,
        out_specs=[APART, APART],
        out_shape=[
            jax.ShapeDtypeStruct(control.shape, BF16),
            jax.ShapeDtypeStruct((sections, slots), F32),
        ],
        scratch_shapes=[
            pltpu.VMEM(control.shape, BF16),
            pltpu.VMEM((sections, slots), F32),
            pltpu.VMEM((2 * mixing.shape[0], 2 * mixing.shape[0]), BF16),
            pltpu.SemaphoreType.DMA((1 + waves_here,)),
        ],
        name="backward_gradient",
        compiler_params=LIMIT,
    )(near(packets), near(grouped), near(control), near(spread), near(mixing))


def make_local(sections, bands):
    def local(
        control, legendre, spectral_sd, vertical, obs_lon, obs_count, kernels, obs_value, obs_weight
    ):
        mixing = vertical[0]
        waves_here, numbers, latitudes = legendre.shape
        levels = mixing.shape[0]
        tile = 2 * waves_here
        terms = tile * bands
        slots = obs_lon.shape[1]
        here = lax.axis_index("section").astype(jnp.int32)
        coeffs = control.reshape(waves_here, 2 * levels, numbers)

        fields = forward_fields(coeffs, legendre, spectral_sd, mixing, sections, bands)
        shares = lax.all_to_all(
            fields.reshape(sections, bands, tile, levels),
            "section", split_axis=0, concat_axis=0, tiled=True,
        )
        field_sum = sum_sections(shares.reshape(sections, terms, levels))
        row_fields = lax.all_to_all(
            field_sum.reshape(bands, tile, levels), "band", split_axis=0, concat_axis=0, tiled=True
        )

        tables = make_basis(
            here[None], obs_count, obs_lon, obs_value, obs_weight, kernels, terms
        )
        grouped = regroup(legendre, sections, bands)
        row_fields, tables, grouped = lax.optimization_barrier((row_fields, tables, grouped))
        by_wave, kern, lines = tables
        adjoint, pieces = observe(
            by_wave, row_fields.reshape(terms, levels), kern, lines, bands
        )
        back = lax.all_to_all(
            adjoint.reshape(bands, tile, levels), "band", split_axis=0, concat_axis=0, tiled=True
        )
        packets = lax.all_to_all(
            pack(back.reshape(terms, levels), pieces, sections, tile),
            "section", split_axis=0, concat_axis=0, tiled=True,
        )
        gradient, all_departures = backward_gradient(
            packets, grouped, coeffs, spectral_sd, mixing, slots
        )
        return (gradient.reshape(control.shape), all_departures)

    return local


def solution(mesh):
    in_specs = (
        P("section", "band", None, None, None),
        P("band", None, None),
        P("section", None),
        P("section", None, None),
        P("band", None),
        P("band"),
        P("band", None, None),
        P("band", None),
        P("band", None),
    )
    out_specs = (P("section", "band", None, None, None), P("band", None))
    local = make_local(mesh.shape["section"], mesh.shape["band"])
    return jax.shard_map(local, mesh=mesh, in_specs=in_specs, out_specs=out_specs, check_vma=False)
```

```python
import functools
import math

import jax
import jax.numpy as jnp
from jax import lax
from jax.experimental import pallas as pl
from jax.experimental.pallas import tpu as pltpu
from jax.sharding import Mesh
from jax.sharding import PartitionSpec as P

NLON = 1024
BAND = ("z", "x", "core")
F32 = jnp.float32
BF16 = jnp.bfloat16
MINOR_BOTH = (((1,), (1,)), ((), ()))


WHOLE = pl.BlockSpec(memory_space=pltpu.VMEM)
SCALAR = pl.BlockSpec(memory_space=pltpu.SMEM)
APART = pl.BlockSpec(memory_space=pl.ANY)


LIMIT = pltpu.CompilerParams(vmem_limit_bytes=16 << 20)


def made(shape, kind):
    return pltpu.VMEM(shape, kind)


def near(array):
    return pltpu.with_memory_space_constraint(array, pltpu.VMEM)


def view(ref, shape):
    return ref.reshape(shape)


def far(array):
    return pltpu.with_memory_space_constraint(array, pltpu.HBM)


def dot(a, b):
    return jnp.dot(a, b, preferred_element_type=F32)


def dot_minor(a, b):
    return lax.dot_general(a, b, MINOR_BOTH, preferred_element_type=F32)


def grouping(grid):
    sections, z, x, cores = grid
    bands = z * x * cores
    size = sections * bands
    place = lax.broadcasted_iota(jnp.int32, (size, size), 0)
    row = lax.broadcasted_iota(jnp.int32, (size, size), 1)
    band = (place // cores % z * x + place // (cores * z) % x) * cores + place % cores
    return jnp.where(sections * band + place // bands == row, 1.0, 0.0).astype(BF16)


def pull(pairs, sems):
    copies = [pltpu.make_async_copy(a, b, sems.at[i]) for i, (a, b) in enumerate(pairs)]
    for copy in copies:
        copy.start()
    return copies


def forward_body(
    grid, control, legendre, spread, mixing, out,
    held, coeffs, basis, spreads, mixings, diagonal, sems,
):
    waves_here, pairs, _ = control.shape
    levels = mixing.shape[0]
    latitudes = legendre.shape[2]
    tile = 2 * waves_here
    order = [(spread, spreads), (mixing, mixings)]
    for m in range(waves_here):
        order += [(control.at[m], coeffs.at[m]), (legendre.at[m], basis.at[m])]
    copies = [pltpu.make_async_copy(a, b, sems.at[i]) for i, (a, b) in enumerate(order)]
    for copy in copies[:6]:
        copy.start()
    copies[0].wait()
    copies[1].wait()
    diagonal[...] = jnp.zeros_like(diagonal)
    for r in range(2):
        part = pl.ds(r * levels, levels)
        diagonal[part, part] = mixings[...]
    for m in range(waves_here):
        copies[2 + 2 * m].wait()
        copies[3 + 2 * m].wait()
        for copy in copies[6 + 2 * m : 8 + 2 * m]:
            copy.start()
        scaled = (coeffs[m].astype(F32) * spreads[...]).astype(BF16)
        rows = lax.dot_general(
            basis[m], scaled, (((0,), (1,)), ((), ())), preferred_element_type=F32
        ).astype(BF16)
        fields = dot_minor(rows, diagonal[...])
        for r in range(2):
            held[pl.ds(2 * m + r, latitudes, stride=tile), :] = fields[
                :, r * levels : (r + 1) * levels
            ]
    sections, z, x, cores = grid
    placed = view(held, (z, x, cores, sections, tile, levels))
    size = z * cores * tile
    for t in range(sections):
        for i in range(x):
            block = placed[:, i, :, t].reshape(size, levels)
            out[pl.ds((t * x + i) * size, size), :] = block.astype(BF16)


def forward_fields(control, legendre, spread, mixing, grid):
    waves_here, pairs, numbers = control.shape
    latitudes = legendre.shape[2]
    levels = mixing.shape[0]
    rows = latitudes * 2 * waves_here
    return pl.pallas_call(
        functools.partial(forward_body, grid),
        in_specs=[APART] * 4,
        out_specs=WHOLE,
        out_shape=made((rows, levels), BF16),
        scratch_shapes=[
            pltpu.VMEM((rows, levels), F32),
            pltpu.VMEM(control.shape, BF16),
            pltpu.VMEM(legendre.shape, BF16),
            pltpu.VMEM(spread.shape, F32),
            pltpu.VMEM(mixing.shape, BF16),
            pltpu.VMEM((2 * levels, 2 * levels), BF16),
            pltpu.SemaphoreType.DMA((2 + 2 * waves_here,)),
        ],
        name="forward_fields",
        compiler_params=LIMIT,
    )(far(control), far(legendre), far(spread), far(mixing))


def turn(index):
    angle = (index & (NLON - 1)).astype(F32) * (2.0 * math.pi / NLON)
    return jnp.cos(angle), jnp.sin(angle)


def basis_body(
    grid, tile, here, at_x, count, obs_lon, value, weight, kernels, by_wave, turned, lines, kern, sems
):
    copy = pull([(kernels.at[here[0]], kern)], sems)[0]
    terms, slots = by_wave.shape
    line = pl.ds(here[0], 1)
    lon = obs_lon[line, :]
    _, z, x, cores = grid
    run = x * cores * tile
    fine = lax.broadcasted_iota(jnp.int32, (run, 1), 0)
    band = (fine // tile) % x * cores + fine // (tile * x)
    wave = band * (tile // 2) + fine % tile // 2
    fine_cos, fine_sin = turn(wave * lon + fine % 2 * (NLON // 4))
    coarse = lax.broadcasted_iota(jnp.int32, (z, 1), 0)
    coarse_cos, coarse_sin = turn(coarse * (run // 2) * lon)
    coarse_cos, coarse_sin = 2.0 * coarse_cos, 2.0 * coarse_sin
    for a in range(z):
        block = coarse_cos[a : a + 1] * fine_cos - coarse_sin[a : a + 1] * fine_sin
        if a == 0:
            block = jnp.where(fine < 2, fine_cos, block)
        by_wave[pl.ds(a * run, run), :] = block.astype(BF16)
    slot = lax.broadcasted_iota(jnp.int32, (1, slots), 1)
    lines[pl.ds(0, 1), :] = value[line, :]
    lines[pl.ds(1, 1), :] = weight[line, :]
    lines[pl.ds(2, 1), :] = jnp.where(slot < count[here[0]], 1.0, 0.0)
    for i in range(x):
        flag = jnp.where(at_x[0] == i, 1.0, 0.0)
        lines[pl.ds(3 + i, 1), :] = jnp.full((1, slots), flag, F32)
    levels = kern.shape[1]
    eye = lax.broadcasted_iota(jnp.int32, (levels, levels), 0) == lax.broadcasted_iota(
        jnp.int32, (levels, levels), 1
    )
    copy.wait()
    turned[...] = dot_minor(jnp.where(eye, 1.0, 0.0).astype(BF16), kern[...]).astype(BF16)


def make_basis(here, at_x, count, obs_lon, value, weight, kernels, terms, grid, tile):
    _, slots, levels = kernels.shape
    return pl.pallas_call(
        functools.partial(basis_body, grid, tile),
        in_specs=[SCALAR, SCALAR, SCALAR, WHOLE, WHOLE, WHOLE, APART],
        out_specs=[WHOLE] * 3,
        out_shape=[
            made((terms, slots), BF16),
            made((levels, slots), BF16),
            made((8, slots), F32),
        ],
        scratch_shapes=[pltpu.VMEM((slots, levels), BF16), pltpu.SemaphoreType.DMA((1,))],
        name="make_basis",
        compiler_params=LIMIT,
    )(here, at_x, count, obs_lon, value, weight, far(kernels))


def observe_body(by_wave, fields, kern, lines, adjoint, pieces, departures):
    columns = dot(fields[...].T, by_wave[...])
    wide = kern[...].astype(F32)
    evolved = jnp.sum(wide * columns, axis=0, keepdims=True)
    departed = jnp.where(lines[pl.ds(2, 1), :] > 0.5, evolved - lines[pl.ds(0, 1), :], 0.0)
    scaled = (lines[pl.ds(1, 1), :] * departed * wide).astype(BF16)
    adjoint[...] = dot_minor(scaled, by_wave[...]).T.astype(BF16)
    size, lanes = departures.shape
    for i in range(size):
        departures[pl.ds(i, 1), :] = departed[:, i * lanes : (i + 1) * lanes]
    rest = departures[...]
    for i in range(3):
        piece = rest.astype(BF16)
        pieces[pl.ds(i * size, size), :] = piece
        rest = rest - piece.astype(F32)


def observe(by_wave, fields, kern, lines):
    levels, slots = kern.shape
    return pl.pallas_call(
        observe_body,
        in_specs=[WHOLE] * 4,
        out_specs=[WHOLE, WHOLE],
        out_shape=[made(fields.shape, BF16), made((3 * slots // levels, levels), BF16)],
        scratch_shapes=[pltpu.VMEM((slots // levels, levels), F32)],
        name="observe",
        compiler_params=LIMIT,
    )(near(by_wave), near(fields), near(kern), near(lines))


def sum_body(parts, out):
    sections, places = parts.shape[:2]
    for i in range(places):
        total = parts[0, i].astype(F32)
        for section in range(1, sections):
            total = total + parts[section, i].astype(F32)
        out[:, i] = total.astype(BF16)


def sum_sections(parts):
    _, places, groups, tile, levels = parts.shape
    return pl.pallas_call(
        sum_body,
        in_specs=[WHOLE],
        out_specs=WHOLE,
        out_shape=made((groups, places, tile, levels), BF16),
        name="sum_sections",
        compiler_params=LIMIT,
    )(near(parts))


def regroup_body(grid, legendre, out):
    group = grouping(grid)
    for m in range(legendre.shape[0]):
        out[m] = dot_minor(group, legendre[m]).astype(BF16)


def regroup(legendre, grid):
    waves_here, numbers, latitudes = legendre.shape
    return pl.pallas_call(
        functools.partial(regroup_body, grid),
        in_specs=[WHOLE],
        out_specs=WHOLE,
        out_shape=jax.ShapeDtypeStruct((waves_here, latitudes, numbers), BF16),
        name="regroup",
        compiler_params=LIMIT,
    )(legendre)


def pack_body(grid, tile, body, pieces, lines, out, held):
    sections, z, x, cores = grid
    held[...] = body[...].astype(F32)
    run = z * cores
    whole = pieces[...].astype(F32)
    for place in range(x):
        for i in range(tile):
            block = held[pl.ds(place * tile + i, run, stride=x * tile), :].astype(BF16)
            for section in range(sections):
                out[section * x + place, pl.ds(i * run, run), :] = block
        own = (whole * lines[pl.ds(3 + place, 1), pl.ds(0, whole.shape[1])]).astype(BF16)
        for section in range(sections):
            out[section * x + place, pl.ds(tile * run, whole.shape[0]), :] = own


def pack(body, pieces, lines, grid, tile):
    sections, z, x, cores = grid
    rows = tile * z * cores + pieces.shape[0]
    return pl.pallas_call(
        functools.partial(pack_body, grid, tile),
        in_specs=[WHOLE, WHOLE, WHOLE],
        out_specs=WHOLE,
        out_shape=made((sections * x, rows, body.shape[1]), BF16),
        scratch_shapes=[pltpu.VMEM(body.shape, F32)],
        name="pack",
        compiler_params=LIMIT,
    )(near(body), near(pieces), near(lines))


def backward_body(
    packets, grouped, control, spread, mixing, out, all_departures,
    ready, departures, diagonal, sems,
):
    origins, _, levels = packets.shape
    waves_here = grouped.shape[0]
    run = grouped.shape[1] // origins
    size = run * 2 * waves_here
    count = departures.shape[1] // levels
    sections = departures.shape[0]
    x = origins // sections
    for t in range(sections):
        parts = []
        for i in range(3):
            part = pl.ds(size + i * count, count)
            own = [packets[t * x + place, part, :].astype(F32) for place in range(x)]
            parts.append(sum(own[1:], own[0]))
        whole = (parts[2] + parts[1]) + parts[0]
        for i in range(count):
            departures[pl.ds(t, 1), pl.ds(i * levels, levels)] = whole[i : i + 1]
    leaving = pull([(departures, all_departures)], sems)
    mixing_t = mixing[...].astype(F32).T.astype(BF16)
    diagonal[...] = jnp.zeros_like(diagonal)
    for r in range(2):
        part = pl.ds(r * levels, levels)
        diagonal[part, part] = mixing_t
    for m in range(waves_here):
        rows = [
            jnp.concatenate([packets[t, pl.ds((2 * m + r) * run, run), :] for t in range(origins)])
            for r in range(2)
        ]
        terms = lax.dot_general(
            jnp.concatenate(rows, axis=1), grouped[m], (((0,), (0,)), ((), ())),
            preferred_element_type=F32,
        ).astype(BF16)
        total = dot(diagonal[...], terms)
        ready[m] = (control[m].astype(F32) + spread[...] * total).astype(BF16)
        copy = pltpu.make_async_copy(ready.at[m], out.at[m], sems.at[m + 1])
        copy.start()
        leaving.append(copy)
    for copy in leaving:
        copy.wait()


def backward_gradient(packets, grouped, control, spread, mixing, sections, slots):
    waves_here = grouped.shape[0]
    return pl.pallas_call(
        backward_body,
        in_specs=[WHOLE] * 5,
        out_specs=[APART, APART],
        out_shape=[
            jax.ShapeDtypeStruct(control.shape, BF16),
            jax.ShapeDtypeStruct((sections, slots), F32),
        ],
        scratch_shapes=[
            pltpu.VMEM(control.shape, BF16),
            pltpu.VMEM((sections, slots), F32),
            pltpu.VMEM((2 * mixing.shape[0], 2 * mixing.shape[0]), BF16),
            pltpu.SemaphoreType.DMA((1 + waves_here,)),
        ],
        name="backward_gradient",
        compiler_params=LIMIT,
    )(near(packets), near(grouped), near(control), near(spread), near(mixing))


def make_local(grid):
    sections, z, x, cores = grid
    bands = z * x * cores

    def local(
        control, legendre, spectral_sd, vertical, obs_lon, obs_count, kernels, obs_value, obs_weight
    ):
        mixing = vertical[0]
        waves_here, numbers, latitudes = legendre.shape
        levels = mixing.shape[0]
        tile = 2 * waves_here
        terms = tile * bands
        slots = obs_lon.shape[1]
        here = lax.axis_index("section").astype(jnp.int32)
        coeffs = control.reshape(waves_here, 2 * levels, numbers)

        fields = forward_fields(coeffs, legendre, spectral_sd, mixing, grid)
        shares = lax.all_to_all(
            fields.reshape(sections * x, z * cores, tile, levels),
            ("section", "x"), split_axis=0, concat_axis=0, tiled=True,
        )
        field_sum = sum_sections(shares.reshape(sections, x, z * cores, tile, levels))
        row_fields = lax.all_to_all(
            field_sum, ("z", "core"), split_axis=0, concat_axis=0, tiled=True
        )
        at_x = lax.axis_index("x").astype(jnp.int32)
        tables = make_basis(
            here[None], at_x[None], obs_count, obs_lon, obs_value, obs_weight, kernels,
            terms, grid, tile,
        )
        grouped = regroup(legendre, grid)
        row_fields, tables, grouped = lax.optimization_barrier((row_fields, tables, grouped))
        by_wave, kern, lines = tables
        adjoint, pieces = observe(by_wave, row_fields.reshape(terms, levels), kern, lines)
        back = lax.all_to_all(
            adjoint.reshape(z * cores, x, tile, levels),
            ("z", "core"), split_axis=0, concat_axis=0, tiled=True,
        )
        packets = lax.all_to_all(
            pack(back.reshape(terms, levels), pieces, lines, grid, tile),
            ("section", "x"), split_axis=0, concat_axis=0, tiled=True,
        )
        gradient, all_departures = backward_gradient(
            packets, grouped, coeffs, spectral_sd, mixing, sections, slots
        )
        return (gradient.reshape(control.shape), all_departures)

    return local


def solution(mesh):
    sections, bands = mesh.shape["section"], mesh.shape["band"]
    cores = 2
    x = min(4, bands // cores)
    z = bands // (cores * x)
    fine_mesh = Mesh(mesh.devices.reshape(sections, z, x, cores), ("section",) + BAND)
    in_specs = (
        P("section", BAND, None, None, None),
        P(BAND, None, None),
        P("section", None),
        P("section", None, None),
        P(BAND, None),
        P(BAND),
        P(BAND, None, None),
        P(BAND, None),
        P(BAND, None),
    )
    out_specs = (P("section", BAND, None, None, None), P(BAND, None))
    local = make_local((sections, z, x, cores))
    return jax.shard_map(
        local, mesh=fine_mesh, in_specs=in_specs, out_specs=out_specs, check_vma=False
    )
```

```python
import functools
import math

import jax
import jax.numpy as jnp
from jax import lax
from jax.experimental import pallas as pl
from jax.experimental.pallas import tpu as pltpu
from jax.sharding import Mesh
from jax.sharding import PartitionSpec as P

NLON = 1024
BAND = ("z", "x", "core")
F32 = jnp.float32
BF16 = jnp.bfloat16
MINOR_BOTH = (((1,), (1,)), ((), ()))


WHOLE = pl.BlockSpec(memory_space=pltpu.VMEM)
SCALAR = pl.BlockSpec(memory_space=pltpu.SMEM)
APART = pl.BlockSpec(memory_space=pl.ANY)


LIMIT = pltpu.CompilerParams(vmem_limit_bytes=16 << 20)


def made(shape, kind):
    return pltpu.VMEM(shape, kind)


def near(array):
    return pltpu.with_memory_space_constraint(array, pltpu.VMEM)


def view(ref, shape):
    return ref.reshape(shape)


def far(array):
    return pltpu.with_memory_space_constraint(array, pltpu.HBM)


def dot(a, b):
    return jnp.dot(a, b, preferred_element_type=F32)


def dot_minor(a, b):
    return lax.dot_general(a, b, MINOR_BOTH, preferred_element_type=F32)


def grouping(grid):
    sections, z, x, cores = grid
    bands = z * x * cores
    size = sections * bands
    place = lax.broadcasted_iota(jnp.int32, (size, size), 0)
    row = lax.broadcasted_iota(jnp.int32, (size, size), 1)
    band = (place // cores % z * x + place // (cores * z) % x) * cores + place % cores
    return jnp.where(sections * band + place // bands == row, 1.0, 0.0).astype(BF16)


def pull(pairs, sems):
    copies = [pltpu.make_async_copy(a, b, sems.at[i]) for i, (a, b) in enumerate(pairs)]
    for copy in copies:
        copy.start()
    return copies


def forward_body(
    grid, control, legendre, spread, mixing, out,
    held, coeffs, basis, spreads, mixings, diagonal, sems,
):
    waves_here, pairs, _ = control.shape
    levels = mixing.shape[0]
    latitudes = legendre.shape[2]
    tile = 2 * waves_here
    order = [(spread, spreads), (mixing, mixings)]
    for m in range(waves_here):
        order += [(control.at[m], coeffs.at[m]), (legendre.at[m], basis.at[m])]
    copies = [pltpu.make_async_copy(a, b, sems.at[i]) for i, (a, b) in enumerate(order)]
    for copy in copies[:6]:
        copy.start()
    copies[0].wait()
    copies[1].wait()
    diagonal[...] = jnp.zeros_like(diagonal)
    for r in range(2):
        part = pl.ds(r * levels, levels)
        diagonal[part, part] = mixings[...]
    for m in range(waves_here):
        copies[2 + 2 * m].wait()
        copies[3 + 2 * m].wait()
        for copy in copies[6 + 2 * m : 8 + 2 * m]:
            copy.start()
        scaled = (coeffs[m].astype(F32) * spreads[...]).astype(BF16)
        rows = lax.dot_general(
            basis[m], scaled, (((0,), (1,)), ((), ())), preferred_element_type=F32
        ).astype(BF16)
        fields = dot_minor(rows, diagonal[...])
        for r in range(2):
            held[pl.ds(2 * m + r, latitudes, stride=tile), :] = fields[
                :, r * levels : (r + 1) * levels
            ]
    sections, z, x, cores = grid
    placed = view(held, (z, x, cores, sections, tile, levels))
    size = z * cores * tile
    for t in range(sections):
        for i in range(x):
            block = placed[:, i, :, t].reshape(size, levels)
            out[pl.ds((t * x + i) * size, size), :] = block.astype(BF16)


def forward_fields(control, legendre, spread, mixing, grid):
    waves_here, pairs, numbers = control.shape
    latitudes = legendre.shape[2]
    levels = mixing.shape[0]
    rows = latitudes * 2 * waves_here
    return pl.pallas_call(
        functools.partial(forward_body, grid),
        in_specs=[APART] * 4,
        out_specs=WHOLE,
        out_shape=made((rows, levels), BF16),
        scratch_shapes=[
            pltpu.VMEM((rows, levels), F32),
            pltpu.VMEM(control.shape, BF16),
            pltpu.VMEM(legendre.shape, BF16),
            pltpu.VMEM(spread.shape, F32),
            pltpu.VMEM(mixing.shape, BF16),
            pltpu.VMEM((2 * levels, 2 * levels), BF16),
            pltpu.SemaphoreType.DMA((2 + 2 * waves_here,)),
        ],
        name="forward_fields",
        compiler_params=LIMIT,
    )(far(control), far(legendre), far(spread), far(mixing))


def turn(index):
    angle = (index & (NLON - 1)).astype(F32) * (2.0 * math.pi / NLON)
    return jnp.cos(angle), jnp.sin(angle)


def basis_body(
    grid, tile, here, at_x, count, obs_lon, value, weight, kernels, by_wave, turned, lines, kern, sems
):
    copy = pull([(kernels.at[here[0]], kern)], sems)[0]
    terms, slots = by_wave.shape
    line = pl.ds(here[0], 1)
    lon = obs_lon[line, :]
    _, z, x, cores = grid
    run = x * cores * tile
    fine = lax.broadcasted_iota(jnp.int32, (run, 1), 0)
    band = (fine // tile) % x * cores + fine // (tile * x)
    wave = band * (tile // 2) + fine % tile // 2
    fine_cos, fine_sin = turn(wave * lon + fine % 2 * (NLON // 4))
    coarse = lax.broadcasted_iota(jnp.int32, (z, 1), 0)
    coarse_cos, coarse_sin = turn(coarse * (run // 2) * lon)
    coarse_cos, coarse_sin = 2.0 * coarse_cos, 2.0 * coarse_sin
    for a in range(z):
        block = coarse_cos[a : a + 1] * fine_cos - coarse_sin[a : a + 1] * fine_sin
        if a == 0:
            block = jnp.where(fine < 2, fine_cos, block)
        by_wave[pl.ds(a * run, run), :] = block.astype(BF16)
    slot = lax.broadcasted_iota(jnp.int32, (1, slots), 1)
    lines[pl.ds(0, 1), :] = value[line, :]
    lines[pl.ds(1, 1), :] = weight[line, :]
    lines[pl.ds(2, 1), :] = jnp.where(slot < count[here[0]], 1.0, 0.0)
    for i in range(x):
        flag = jnp.where(at_x[0] == i, 1.0, 0.0)
        lines[pl.ds(3 + i, 1), :] = jnp.full((1, slots), flag, F32)
    levels = kern.shape[1]
    eye = lax.broadcasted_iota(jnp.int32, (levels, levels), 0) == lax.broadcasted_iota(
        jnp.int32, (levels, levels), 1
    )
    copy.wait()
    turned[...] = dot_minor(jnp.where(eye, 1.0, 0.0).astype(BF16), kern[...]).astype(BF16)


def make_basis(here, at_x, count, obs_lon, value, weight, kernels, terms, grid, tile):
    _, slots, levels = kernels.shape
    return pl.pallas_call(
        functools.partial(basis_body, grid, tile),
        in_specs=[SCALAR, SCALAR, SCALAR, WHOLE, WHOLE, WHOLE, APART],
        out_specs=[WHOLE] * 3,
        out_shape=[
            made((terms, slots), BF16),
            made((levels, slots), BF16),
            made((8, slots), F32),
        ],
        scratch_shapes=[pltpu.VMEM((slots, levels), BF16), pltpu.SemaphoreType.DMA((1,))],
        name="make_basis",
        compiler_params=LIMIT,
    )(here, at_x, count, obs_lon, value, weight, far(kernels))


def observe_body(by_wave, fields, kern, lines, adjoint, pieces, departures):
    columns = dot(fields[...].T, by_wave[...])
    wide = kern[...].astype(F32)
    evolved = jnp.sum(wide * columns, axis=0, keepdims=True)
    departed = jnp.where(lines[pl.ds(2, 1), :] > 0.5, evolved - lines[pl.ds(0, 1), :], 0.0)
    scaled = (lines[pl.ds(1, 1), :] * departed * wide).astype(BF16)
    adjoint[...] = dot_minor(scaled, by_wave[...]).T.astype(BF16)
    size, lanes = departures.shape
    for i in range(size):
        departures[pl.ds(i, 1), :] = departed[:, i * lanes : (i + 1) * lanes]
    rest = departures[...]
    for i in range(3):
        piece = rest.astype(BF16)
        pieces[pl.ds(i * size, size), :] = piece
        rest = rest - piece.astype(F32)


def observe(by_wave, fields, kern, lines):
    levels, slots = kern.shape
    return pl.pallas_call(
        observe_body,
        in_specs=[WHOLE] * 4,
        out_specs=[WHOLE, WHOLE],
        out_shape=[made(fields.shape, BF16), made((3 * slots // levels, levels), BF16)],
        scratch_shapes=[pltpu.VMEM((slots // levels, levels), F32)],
        name="observe",
        compiler_params=LIMIT,
    )(near(by_wave), near(fields), near(kern), near(lines))


def sum_body(parts, out):
    sections, places = parts.shape[:2]
    for i in range(places):
        total = parts[0, i].astype(F32)
        for section in range(1, sections):
            total = total + parts[section, i].astype(F32)
        out[:, i] = total.astype(BF16)


def sum_sections(parts):
    _, places, groups, tile, levels = parts.shape
    return pl.pallas_call(
        sum_body,
        in_specs=[WHOLE],
        out_specs=WHOLE,
        out_shape=made((groups, places, tile, levels), BF16),
        name="sum_sections",
        compiler_params=LIMIT,
    )(near(parts))


def regroup_body(grid, legendre, out):
    group = grouping(grid)
    for m in range(legendre.shape[0]):
        out[m] = dot_minor(group, legendre[m]).astype(BF16)


def regroup(legendre, grid):
    waves_here, numbers, latitudes = legendre.shape
    return pl.pallas_call(
        functools.partial(regroup_body, grid),
        in_specs=[WHOLE],
        out_specs=WHOLE,
        out_shape=jax.ShapeDtypeStruct((waves_here, latitudes, numbers), BF16),
        name="regroup",
        compiler_params=LIMIT,
    )(legendre)


def pack_body(grid, tile, body, pieces, lines, out, held):
    sections, z, x, cores = grid
    held[...] = body[...].astype(F32)
    run = z * cores
    whole = pieces[...].astype(F32)
    for place in range(x):
        for i in range(tile):
            block = held[pl.ds(place * tile + i, run, stride=x * tile), :].astype(BF16)
            for section in range(sections):
                out[section * x + place, pl.ds(i * run, run), :] = block
        own = (whole * lines[pl.ds(3 + place, 1), pl.ds(0, whole.shape[1])]).astype(BF16)
        for section in range(sections):
            out[section * x + place, pl.ds(tile * run, whole.shape[0]), :] = own


def pack(body, pieces, lines, grid, tile):
    sections, z, x, cores = grid
    rows = tile * z * cores + pieces.shape[0]
    return pl.pallas_call(
        functools.partial(pack_body, grid, tile),
        in_specs=[WHOLE, WHOLE, WHOLE],
        out_specs=WHOLE,
        out_shape=made((sections * x, rows, body.shape[1]), BF16),
        scratch_shapes=[pltpu.VMEM(body.shape, F32)],
        name="pack",
        compiler_params=LIMIT,
    )(near(body), near(pieces), near(lines))


def backward_body(
    packets, grouped, control, spread, mixing, out, all_departures,
    ready, departures, diagonal, sems,
):
    origins, _, levels = packets.shape
    waves_here = grouped.shape[0]
    run = grouped.shape[1] // origins
    size = run * 2 * waves_here
    count = departures.shape[1] // levels
    sections = departures.shape[0]
    x = origins // sections
    leaving = []
    mixing_t = mixing[...].astype(F32).T.astype(BF16)
    diagonal[...] = jnp.zeros_like(diagonal)
    for r in range(2):
        part = pl.ds(r * levels, levels)
        diagonal[part, part] = mixing_t
    for m in range(waves_here):
        rows = [
            jnp.concatenate([packets[t, pl.ds((2 * m + r) * run, run), :] for t in range(origins)])
            for r in range(2)
        ]
        terms = lax.dot_general(
            jnp.concatenate(rows, axis=1), grouped[m], (((0,), (0,)), ((), ())),
            preferred_element_type=F32,
        ).astype(BF16)
        total = dot(diagonal[...], terms)
        ready[m] = (control[m].astype(F32) + spread[...] * total).astype(BF16)
        copy = pltpu.make_async_copy(ready.at[m], out.at[m], sems.at[m + 1])
        copy.start()
        leaving.append(copy)
        if m == 0:
            for t in range(sections):
                parts = []
                for i in range(3):
                    part = pl.ds(size + i * count, count)
                    own = [packets[t * x + place, part, :].astype(F32) for place in range(x)]
                    parts.append(sum(own[1:], own[0]))
                whole = (parts[2] + parts[1]) + parts[0]
                for i in range(count):
                    departures[pl.ds(t, 1), pl.ds(i * levels, levels)] = whole[i : i + 1]
            leaving += pull([(departures, all_departures)], sems)
    for copy in leaving:
        copy.wait()


def backward_gradient(packets, grouped, control, spread, mixing, sections, slots):
    waves_here = grouped.shape[0]
    return pl.pallas_call(
        backward_body,
        in_specs=[WHOLE] * 5,
        out_specs=[APART, APART],
        out_shape=[
            jax.ShapeDtypeStruct(control.shape, BF16),
            jax.ShapeDtypeStruct((sections, slots), F32),
        ],
        scratch_shapes=[
            pltpu.VMEM(control.shape, BF16),
            pltpu.VMEM((sections, slots), F32),
            pltpu.VMEM((2 * mixing.shape[0], 2 * mixing.shape[0]), BF16),
            pltpu.SemaphoreType.DMA((1 + waves_here,)),
        ],
        name="backward_gradient",
        compiler_params=LIMIT,
    )(near(packets), near(grouped), near(control), near(spread), near(mixing))


def make_local(grid):
    sections, z, x, cores = grid
    bands = z * x * cores

    def local(
        control, legendre, spectral_sd, vertical, obs_lon, obs_count, kernels, obs_value, obs_weight
    ):
        mixing = vertical[0]
        waves_here, numbers, latitudes = legendre.shape
        levels = mixing.shape[0]
        tile = 2 * waves_here
        terms = tile * bands
        slots = obs_lon.shape[1]
        here = lax.axis_index("section").astype(jnp.int32)
        coeffs = control.reshape(waves_here, 2 * levels, numbers)

        fields = forward_fields(coeffs, legendre, spectral_sd, mixing, grid)
        shares = lax.all_to_all(
            fields.reshape(sections * x, z * cores, tile, levels),
            ("section", "x"), split_axis=0, concat_axis=0, tiled=True,
        )
        field_sum = sum_sections(shares.reshape(sections, x, z * cores, tile, levels))
        row_fields = lax.all_to_all(
            field_sum, ("z", "core"), split_axis=0, concat_axis=0, tiled=True
        )
        at_x = lax.axis_index("x").astype(jnp.int32)
        tables = make_basis(
            here[None], at_x[None], obs_count, obs_lon, obs_value, obs_weight, kernels,
            terms, grid, tile,
        )
        grouped = regroup(legendre, grid)
        row_fields, tables, grouped = lax.optimization_barrier((row_fields, tables, grouped))
        by_wave, kern, lines = tables
        adjoint, pieces = observe(by_wave, row_fields.reshape(terms, levels), kern, lines)
        back = lax.all_to_all(
            adjoint.reshape(z * cores, x, tile, levels),
            ("z", "core"), split_axis=0, concat_axis=0, tiled=True,
        )
        packets = lax.all_to_all(
            pack(back.reshape(terms, levels), pieces, lines, grid, tile),
            ("section", "x"), split_axis=0, concat_axis=0, tiled=True,
        )
        gradient, all_departures = backward_gradient(
            packets, grouped, coeffs, spectral_sd, mixing, sections, slots
        )
        return (gradient.reshape(control.shape), all_departures)

    return local


def solution(mesh):
    sections, bands = mesh.shape["section"], mesh.shape["band"]
    cores = 2
    x = min(4, bands // cores)
    z = bands // (cores * x)
    fine_mesh = Mesh(mesh.devices.reshape(sections, z, x, cores), ("section",) + BAND)
    in_specs = (
        P("section", BAND, None, None, None),
        P(BAND, None, None),
        P("section", None),
        P("section", None, None),
        P(BAND, None),
        P(BAND),
        P(BAND, None, None),
        P(BAND, None),
        P(BAND, None),
    )
    out_specs = (P("section", BAND, None, None, None), P(BAND, None))
    local = make_local((sections, z, x, cores))
    return jax.shard_map(
        local, mesh=fine_mesh, in_specs=in_specs, out_specs=out_specs, check_vma=False
    )
```
